32 devices in a mesh: hi: 4 (over z), lo: 8 (over y, x, core).
Axes of the slice: x: 2, y: 2, z: 4, core: 2. Of those that a mesh axis runs over, the one named last changes fastest.
Arguments:
- ket_state: float32 [2, 2097152], P(None, ('hi', 'lo')), may hold values from -6 to 6
- bra_state: float32 [2, 2097152], P(None, ('hi', 'lo')), may hold values from -6 to 6
- gates: float32 [4, 4, 2, 128, 128], replicated, may hold values from -0.375 to 0.375
- targets: int32 [4, 4, 128], replicated, may hold values from 0 to 127, each once within a row
- swap_order: int32 [4, 8], replicated, may hold values from 0 to 7, each once within a row
Outputs:
- ket_final: float32 [2, 2097152], P(None, ('hi', 'lo'))
- bra_final: float32 [2, 2097152], P(None, ('hi', 'lo'))
- gate_grads: float32 [4, 4, 2, 128, 128], P(None, None, None, 'hi')
The draws below stay inside these ranges and needn't reach their ends.
Inputs may be any that keep to these rules, and one draw needn't show every extreme that they name: Each row of targets holds every value once. Each row of swap_order holds every value once.
All inputs are finite; a program needn't handle non-finite values.
Results may differ from the reference program's by a relative error of at most 0.00015.
Values sent between devices are 32-bit elements; how exact they have to be, the bound alone decides.
A program may use at most 64 MiB of HBM per device.

```python
import jax
import jax.numpy as jnp
from jax import lax

GATE_DIM = 128
LAYERS = 4
GATES = 4
AMPS = 2097152
SWAPPED = 8
N_HI = 4
N_LO = 8


def shard_levels(rng, extent, shards, least, top_value):
    factor_of, own = 1.0, jax.random.fold_in(rng, 6)
    for dim, shards_of in shards:
        steps = jnp.exp(jax.random.uniform(jax.random.fold_in(own, dim), (shards_of,), jnp.float32, least / len(shards), top_value / len(shards)))
        factor_of = factor_of * jnp.repeat(steps, extent[dim] // shards_of).reshape([-1 if axis == dim else 1 for axis in range(len(extent))])
    return factor_of


def normal_values(rng, shape, width, reach, shards=(), kind=jnp.bfloat16):
    array = width * jax.random.normal(rng, shape, jnp.float32)
    if shards:
        array = array * shard_levels(rng, shape, shards, -0.22, 0.18)
    return jnp.clip(array, -reach, reach).astype(kind)


def setup_inputs(seed: int = 0) -> dict:
    key_of = jax.random.split(jax.random.key(seed), 6)
    ket_state = normal_values(key_of[0], (2, AMPS), 1.0, 6.0, ((1, 32),), jnp.float32)
    bra_state = normal_values(key_of[1], (2, AMPS), 1.0, 6.0, ((1, 32),), jnp.float32)
    gates = normal_values(key_of[2], (LAYERS, GATES, 2, GATE_DIM, GATE_DIM), (2 * GATE_DIM) ** -0.5, 0.375, (), jnp.float32)
    targets = jax.vmap(lambda own: jax.random.permutation(own, GATE_DIM))(jax.random.split(key_of[3], LAYERS * GATES)).reshape((LAYERS, GATES, GATE_DIM)).astype(jnp.int32)
    swap_order = jax.vmap(lambda own: jax.random.permutation(own, SWAPPED))(jax.random.split(key_of[4], LAYERS)).reshape((LAYERS, SWAPPED)).astype(jnp.int32)
    return {"ket_state": ket_state, "bra_state": bra_state, "gates": gates, "targets": targets, "swap_order": swap_order}


exact_mode = lax.Precision.HIGHEST

def relabel(gate_matrix, ordering):
    return jnp.take(jnp.take(gate_matrix, ordering, axis=1), ordering, axis=2)

def right_apply(amplitudes, gate_matrix):
    real_part = jnp.einsum('...j,ij->...i', amplitudes[0], gate_matrix[0], precision=exact_mode) - jnp.einsum('...j,ij->...i', amplitudes[1], gate_matrix[1], precision=exact_mode)
    imag_part = jnp.einsum('...j,ij->...i', amplitudes[0], gate_matrix[1], precision=exact_mode) + jnp.einsum('...j,ij->...i', amplitudes[1], gate_matrix[0], precision=exact_mode)
    return jnp.stack([real_part, imag_part])

def left_apply(amplitudes, gate_matrix):
    real_part = jnp.einsum('ij,djr->dir', gate_matrix[0], amplitudes[0], precision=exact_mode) - jnp.einsum('ij,djr->dir', gate_matrix[1], amplitudes[1], precision=exact_mode)
    imag_part = jnp.einsum('ij,djr->dir', gate_matrix[1], amplitudes[0], precision=exact_mode) + jnp.einsum('ij,djr->dir', gate_matrix[0], amplitudes[1], precision=exact_mode)
    return jnp.stack([real_part, imag_part])

def low_grad(bra_view, ket_view):
    real_part = jnp.einsum('ri,rj->ij', bra_view[0], ket_view[0], precision=exact_mode) + jnp.einsum('ri,rj->ij', bra_view[1], ket_view[1], precision=exact_mode)
    imag_part = jnp.einsum('ri,rj->ij', bra_view[1], ket_view[0], precision=exact_mode) - jnp.einsum('ri,rj->ij', bra_view[0], ket_view[1], precision=exact_mode)
    return jnp.stack([real_part, imag_part])

def high_grad(bra_view, ket_view):
    real_part = jnp.einsum('dir,djr->ij', bra_view[0], ket_view[0], precision=exact_mode) + jnp.einsum('dir,djr->ij', bra_view[1], ket_view[1], precision=exact_mode)
    imag_part = jnp.einsum('dir,djr->ij', bra_view[1], ket_view[0], precision=exact_mode) - jnp.einsum('dir,djr->ij', bra_view[0], ket_view[1], precision=exact_mode)
    return jnp.stack([real_part, imag_part])

def advance(ket_state, bra_state, gate_matrix, kind, devices):
    gate_width = gate_matrix.shape[-1]
    if kind == 0:
        ket_view = ket_state.reshape(2, -1, gate_width)
        bra_view = bra_state.reshape(2, -1, gate_width)
        ket_next = right_apply(ket_view, gate_matrix)
        gradient = low_grad(bra_view, ket_next)
        bra_next = right_apply(bra_view, gate_matrix)
    else:
        ket_view = ket_state.reshape(2, devices, gate_width, -1)
        bra_view = bra_state.reshape(2, devices, gate_width, -1)
        ket_next = left_apply(ket_view, gate_matrix)
        gradient = high_grad(bra_view, ket_next)
        bra_next = left_apply(bra_view, gate_matrix)
    return (ket_next.reshape(ket_state.shape), bra_next.reshape(bra_state.shape), gradient)

def swap_global(amplitudes, ordering):
    viewed = amplitudes.reshape(2, N_HI, N_LO, N_LO, -1)
    viewed = jnp.take(viewed, ordering, axis=3)
    viewed = jnp.swapaxes(viewed, 2, 3)
    return viewed.reshape(2, AMPS)

def reference(ket_state, bra_state, gates, targets, swap_order):
    devices_all = N_HI * N_LO
    grad_scale = (AMPS // GATE_DIM) ** (-0.5)
    collected = []
    for layer_index in range(LAYERS):
        for gate_index in range(GATES):
            gate_matrix = relabel(gates[layer_index, gate_index], targets[layer_index, gate_index])
            ket_state, bra_state, gradient = advance(ket_state, bra_state, gate_matrix, gate_index % 2, devices_all)
            collected.append(gradient * grad_scale)
        ket_state = swap_global(ket_state, swap_order[layer_index])
        bra_state = swap_global(bra_state, swap_order[layer_index])
    all_grads = jnp.stack(collected).reshape(LAYERS, GATES, 2, GATE_DIM, GATE_DIM)
    return (ket_state, bra_state, all_grads)
```

```python
import functools

import jax
import jax.numpy as jnp
from jax import lax
from jax.experimental import pallas as pl
from jax.experimental.pallas import tpu as pltpu
from jax.sharding import PartitionSpec as P

bf16 = jnp.bfloat16
f32 = jnp.float32


def split(x):
    high = x.astype(bf16)
    return high, (x - high.astype(f32)).astype(bf16)


def mm(a, b):
    return lax.dot_general(a, b, (((1,), (0,)), ((), ())), preferred_element_type=f32)


def mm_nt(a, b):
    return lax.dot_general(a, b, (((1,), (1,)), ((), ())), preferred_element_type=f32)


def block_swap(x):
    r, c = x.shape[0] // 2, x.shape[1] // 2
    return jnp.concatenate(
        [
            jnp.concatenate([x[:r, :c], x[r:, :c]], axis=1),
            jnp.concatenate([x[:r, c:], x[r:, c:]], axis=1),
        ],
        axis=0,
    )


def kernel(
    n_hi, n_lo, layers, gate_count, chunks, width, scale,
    sigma_ref, ket_hbm, bra_hbm, gates_hbm, targets_ref, ket_out, bra_out, grad_hbm,
    ket_ref, bra_ref, rbuf, sbuf, ybuf, vbuf, tape_b, tape_even, tape_odd,
    acc, r0buf, hsum, r1buf, p1, r2buf, x1buf, x2, x2buf, gout,
    gates_ref, in_sem, out_sem, gather_s, gather_r, trade_s, trade_r, home_s, home_r,
    s0, q0, s1, q1, s2, q2, s3, q3,
):
    h = lax.axis_index("hi")
    q = lax.axis_index("lo")
    core = lax.rem(q, 2)
    chip = q // 2
    n_chip = n_lo // 2
    half = gate_count // 2
    rows = width // n_hi
    piece = rows // n_chip
    w2 = 2 * width
    last = layers - 1

    def lo_peer(k):
        return lax.rem(q + k, n_lo)

    def hi_peer(k):
        return lax.rem(h + k, n_hi)

    def chip_peer(k):
        peer, bit = 0, 1
        while bit < n_chip:
            own = lax.rem(chip // bit, 2)
            peer = peer + bit * (1 - own if k & bit else own)
            bit *= 2
        return peer

    in_copies = [
        pltpu.make_async_copy(gates_hbm.at[0], gates_ref.at[0], in_sem.at[0]),
        pltpu.make_async_copy(ket_hbm, ket_ref, in_sem.at[1]),
        pltpu.make_async_copy(bra_hbm, bra_ref, in_sem.at[2]),
        pltpu.make_async_copy(
            gates_hbm.at[pl.ds(1, last)], gates_ref.at[pl.ds(1, last)], in_sem.at[3]
        ),
    ]
    for copy in in_copies:
        copy.start()

    barrier = pltpu.get_barrier_semaphore()
    for k in range(1, n_lo):
        pl.semaphore_signal(barrier, inc=1, device_id={"lo": lo_peer(k)})
    for k in range(1, n_hi):
        pl.semaphore_signal(barrier, inc=1, device_id={"hi": hi_peer(k)})

    def entering(m):
        parts = [
            jnp.concatenate(
                [v[pl.ds(2 * m + c, width, stride=2 * chunks), :] for v in (ket_ref, bra_ref)], axis=1
            )
            for c in range(2)
        ]
        return jnp.concatenate(parts, axis=0)

    def prepare(layer, gate):
        order = targets_ref[layer, gate]
        picks = (
            jnp.broadcast_to(order, (width, width))
            == lax.broadcasted_iota(jnp.int32, (width, width), 0)
        ).astype(f32)
        rows_pick = picks.T.astype(bf16)
        g = gates_ref[layer, gate]
        rh, rl = split(g[0])
        ih, il = split(g[1])
        t = mm(jnp.concatenate([rh, ih, rl, il], axis=0), picks.astype(bf16)).astype(bf16)
        w = mm(
            rows_pick,
            jnp.concatenate([t[i * width:(i + 1) * width] for i in range(4)], axis=1),
        ).astype(bf16)
        wrh, wih, wrl, wil = [w[:, i * width:(i + 1) * width] for i in range(4)]
        vbuf[layer, gate] = jnp.concatenate(
            [
                jnp.concatenate([wrh, -wih, wrh, -wih, wrl, -wil], axis=1),
                jnp.concatenate([wih, wrh, wih, wrh, wil, wrl], axis=1),
            ],
            axis=0,
        )

    chip_order = list(range(n_chip - 1, -1, -1))
    targets_order = [(kc, ke) for kc in chip_order for ke in (1, 0)]
    others = [pair for pair in targets_order if pair != (0, 0)]
    part = chunks // 2

    def gather_copy(kc, ke, p, incoming=False):
        m, e = chip_peer(kc), lax.rem(core + ke, 2)
        d = 2 * m + e
        return pltpu.make_async_remote_copy(
            src_ref=sbuf.at[0, m, pl.ds(chunks * e + part * p, part)],
            dst_ref=rbuf.at[1, pl.ds(part * p, part), :, d if incoming else q],
            send_sem=gather_s.at[p, d],
            recv_sem=gather_r.at[p, d if incoming else q],
            device_id={"lo": d},
        )

    def trade_copy(l, i, incoming=False):
        return pltpu.make_async_remote_copy(
            src_ref=sbuf.at[l, i, pl.ds(0, chunks)],
            dst_ref=rbuf.at[l + 1, :, :, 2 * i + (1 - core if incoming else core)],
            send_sem=trade_s.at[l, i],
            recv_sem=trade_r.at[l, i],
            device_id={"lo": q + 1 - 2 * core},
        )

    def home_copy(i, kc, ke, incoming=False):
        m, e = chip_peer(kc), lax.rem(core + ke, 2)
        d = 2 * m + e
        return pltpu.make_async_remote_copy(
            src_ref=sbuf.at[last, i, d],
            dst_ref=rbuf.at[layers, m if incoming else chip, :, 2 * i + (e if incoming else core)],
            send_sem=home_s.at[i, d],
            recv_sem=home_r.at[i, d if incoming else q],
            device_id={"lo": d},
        )

    def r0_copy(l):
        return pltpu.make_async_remote_copy(
            src_ref=acc.at[l, pl.ds(half * (1 - core), half)],
            dst_ref=r0buf.at[l],
            send_sem=s0.at[l],
            recv_sem=q0.at[l],
            device_id={"lo": q + 1 - 2 * core},
        )

    lo_first = (1,)

    def hi_copy(l, k, incoming=False):
        d = hi_peer(k)
        if l in lo_first:
            src, dst = x2.at[l, :, :, d], x2buf.at[l, d if incoming else h]
        else:
            src, dst = hsum.at[l, :, :, d], r1buf.at[l, d if incoming else h]
        return pltpu.make_async_remote_copy(
            src_ref=src,
            dst_ref=dst,
            send_sem=s1.at[l, d],
            recv_sem=q1.at[l, d if incoming else h],
            device_id={"hi": d},
        )

    def chip_copy(l, k, incoming=False):
        d = chip_peer(k)
        if l in lo_first:
            src, dst = hsum.at[l, :, :, :, d], x1buf.at[l, d if incoming else chip]
        else:
            src, dst = p1.at[l, :, :, d], r2buf.at[l, d if incoming else chip]
        return pltpu.make_async_remote_copy(
            src_ref=src,
            dst_ref=dst,
            send_sem=s2.at[l, d],
            recv_sem=q2.at[l, d if incoming else chip],
            device_id={"lo": 2 * d + core},
        )

    def r3_copy(l, k, incoming=False):
        d = lo_peer(k)
        owner = d if incoming else q
        place = gout.at[l, pl.ds(half * lax.rem(owner, 2), half), :, owner // 2]
        return pltpu.make_async_remote_copy(
            src_ref=place,
            dst_ref=place,
            send_sem=s3.at[l, d],
            recv_sem=q3.at[l, owner],
            device_id={"lo": d},
        )

    def hi_start(l):
        for k in range(n_hi - 1, 0, -1):
            hi_copy(l, k).start()

    def chip_start(l):
        for k in range(n_chip - 1, 0, -1):
            chip_copy(l, k).start()

    def stage0(l):
        r0_copy(l).wait_recv()
        total = acc[l, pl.ds(half * core, half)] + r0buf[l]
        hsum[l] = total.reshape(half, 2, n_hi, n_chip, piece, width)
        if l in lo_first:
            chip_start(l)
        else:
            hi_start(l)

    def stage1(l):
        if l in lo_first:
            total = hsum[l, :, :, :, chip]
            for k in range(1, n_chip):
                chip_copy(l, k, True).wait_recv()
                total = total + x1buf[l, chip_peer(k)]
            x2[l] = total
            hi_start(l)
        else:
            total = hsum[l, :, :, h]
            for k in range(1, n_hi):
                hi_copy(l, k, True).wait_recv()
                total = total + r1buf[l, hi_peer(k)]
            p1[l] = total
            chip_start(l)

    def stage2(l):
        if l in lo_first:
            total = x2[l, :, :, h]
            for k in range(1, n_hi):
                hi_copy(l, k, True).wait_recv()
                total = total + x2buf[l, hi_peer(k)]
        else:
            total = p1[l, :, :, chip]
            for k in range(1, n_chip):
                chip_copy(l, k, True).wait_recv()
                total = total + r2buf[l, chip_peer(k)]
        gout[l, pl.ds(half * core, half), :, chip] = total * scale
        for k in range(n_lo - 1, 0, -1):
            r3_copy(l, k).start()

    def grad_out(l):
        return pltpu.make_async_copy(gout.at[l], grad_hbm.at[l], out_sem.at[2 + l])

    def stage3(l):
        for k in range(1, n_lo):
            r3_copy(l, k, True).wait_recv()
        grad_out(l).start()

    def cat(v, axis):
        return jnp.concatenate(v, axis=axis) if len(v) > 1 else v[0]

    def apply_gates(ss, l, first):
        n = len(ss)
        hs, ls = zip(*[split(s) for s in ss])
        spans = [slice((first + i) * width, (first + i + 1) * width) for i in range(n)]
        for g in range(gate_count):
            v = vbuf[l, g]
            if g % 2 == 0:
                xh = cat([block_swap(t) for t in hs], 0)
                xl = cat([block_swap(t) for t in ls], 0)
                y = mm_nt(cat([xh, xl, xh], 1), v)
                ys = [y[i * w2:(i + 1) * w2] for i in range(n)]
                yhs, yls = zip(*[split(t) for t in ys])
                for s, yh, yl, span in zip(ss, yhs, yls, spans):
                    bh, bl = split(cat([s[:width, width:], s[width:, width:]], 1).T)
                    tape_b[g, 0, :, span] = bh
                    tape_b[g, 1, :, span] = bl
                    tape_even[g // 2, 0, span, :] = yh[:width]
                    tape_even[g // 2, 1, span, :] = yl[:width]
                ss = [block_swap(t) for t in ys]
                hs = [block_swap(t) for t in yhs]
                ls = [block_swap(t) for t in yls]
            else:
                sh, sl = cat(hs, 1), cat(ls, 1)
                y = mm(v, cat([sh, sl, sh], 0))
                ys = [y[:, i * w2:(i + 1) * w2] for i in range(n)]
                yhs, yls = zip(*[split(t) for t in ys])
                for sh, sl, yh, yl, span in zip(hs, ls, yhs, yls, spans):
                    tape_b[g, 0, :, span] = sh[:, width:]
                    tape_b[g, 1, :, span] = sl[:, width:]
                    tape_odd[g // 2, 0, :, span] = yh[:, :width]
                    tape_odd[g // 2, 1, :, span] = yl[:, :width]
                ss, hs, ls = ys, yhs, yls
        return ss

    def gradients(l):
        @pl.loop(0, half)
        def _(pair):
            for odd in range(2):
                g = 2 * pair + odd
                bh, bl = tape_b[g, 0], tape_b[g, 1]
                b = cat([bh, bh, bl], 1)
                if odd:
                    kh, kl = tape_odd[pair, 0], tape_odd[pair, 1]
                    grad = mm_nt(b, cat([kh, kl, kh], 1))
                else:
                    kh, kl = tape_even[pair, 0], tape_even[pair, 1]
                    grad = mm(b, cat([kh, kl, kh], 0))
                acc[l, g, 0] = grad[:width, :width] + grad[width:, width:]
                acc[l, g, 1] = grad[width:, :width] - grad[:width, width:]

        r0_copy(l).start()

    def load(l, i):
        return rbuf[l, i].reshape(w2, w2)

    in_copies[0].wait()
    for g in range(gate_count):
        prepare(0, g)
    in_copies[1].wait()
    in_copies[2].wait()
    done = 0
    for todo in (chip_order[:1], chip_order[1:]):
        states = apply_gates([entering(chip_peer(kc)) for kc in todo], 0, done)
        done += len(todo)
        for kc, state in zip(todo, states):
            ybuf[kc] = state.reshape(ybuf.shape[1:])
        if todo[0] == chip_order[0]:
            pl.semaphore_wait(barrier, n_lo - 1 + n_hi - 1)
        for p in range(2):
            for kc in todo:
                m = chip_peer(kc)
                for ke in (1, 0):
                    e = lax.rem(core + ke, 2)
                    for j in range(part * p, part * (p + 1)):
                        block = ybuf[kc, :, sigma_ref[0, 2 * j + e]]
                        if (kc, ke) == (0, 0):
                            rbuf[1, j, :, q] = block
                        else:
                            sbuf[0, m, chunks * e + j] = block
                    if (kc, ke) != (0, 0):
                        gather_copy(kc, ke, p).start()
    gradients(0)
    in_copies[3].wait()

    def prepare_layers(first, end):
        @pl.loop(first, end)
        def _(l):
            for g in range(gate_count):
                prepare(l, g)

    prepare_layers(1, 2)
    stage0(0)
    prepare_layers(2, layers)

    for l in range(1, last):
        for p in range(2):
            if l == 1:
                for kc, ke in others:
                    gather_copy(kc, ke, p, True).wait_recv()
            elif p == 0:
                for i in range(chunks):
                    trade_copy(l - 1, i, True).wait_recv()
            todo = range(part * p, part * (p + 1))
            states = apply_gates([load(l, i) for i in todo], l, part * p)
            for i, state in zip(todo, states):
                ybuf[i] = state.reshape(ybuf.shape[1:])
                for j in range(chunks):
                    sbuf[l, i, j] = ybuf[i, :, sigma_ref[l, 2 * j + 1 - core]]
                trade_copy(l, i).start()
                for j in range(chunks):
                    rbuf[l + 1, j, :, 2 * i + core] = ybuf[i, :, sigma_ref[l, 2 * j + core]]
            if l > 1 and p == 0:
                stage0(l - 1)
        if l == 1:
            stage1(0)
        else:
            stage2(l - 2)
            stage1(l - 1)
        gradients(l)

    for i in range(chunks):
        trade_copy(last - 1, i, True).wait_recv()
    for todo in ([0], range(1, chunks)):
        states = apply_gates([load(last, i) for i in todo], last, todo[0])
        for i, state in zip(todo, states):
            ybuf[i] = state.reshape(ybuf.shape[1:])
            for kc, ke in targets_order:
                d = 2 * chip_peer(kc) + lax.rem(core + ke, 2)
                block = ybuf[i, :, sigma_ref[last, d]]
                if (kc, ke) == (0, 0):
                    rbuf[layers, chip, :, 2 * i + core] = block
                else:
                    sbuf[last, i, d] = block
                    home_copy(i, kc, ke).start()
        if todo[0] == 0:
            stage0(last - 1)
    gradients(last)
    stage2(last - 2)
    stage0(last)
    stage1(last - 1)
    for l in range(last - 2):
        stage3(l)

    for kc in [0] + [k for k in chip_order if k]:
        for ke in (1, 0):
            if (kc, ke) != (0, 0):
                for i in range(chunks):
                    home_copy(i, kc, ke, True).wait_recv()
        m = chip_peer(kc)
        state = load(layers, m)
        for c in range(2):
            for n, out in enumerate((ket_ref, bra_ref)):
                out[pl.ds(2 * m + c, width, stride=2 * chunks), :] = state[
                    c * width:(c + 1) * width, n * width:(n + 1) * width
                ]
    state_out = [
        pltpu.make_async_copy(ket_ref, ket_out, out_sem.at[0]),
        pltpu.make_async_copy(bra_ref, bra_out, out_sem.at[1]),
    ]
    for copy in state_out:
        copy.start()

    stage1(last)
    stage2(last - 1)
    stage2(last)
    for l in range(last - 2, layers):
        stage3(l)

    for kc, ke in others:
        for p in range(2):
            gather_copy(kc, ke, p).wait_send()

    @pl.loop(0, chunks)
    def _(i):
        for kc, ke in others:
            home_copy(i, kc, ke).wait_send()

        @pl.loop(1, last)
        def _(l):
            trade_copy(l, i).wait_send()

    for l in range(layers):
        r0_copy(l).wait_send()
        for k in range(1, n_hi):
            hi_copy(l, k).wait_send()
        for k in range(1, n_chip):
            chip_copy(l, k).wait_send()
        for k in range(1, n_lo):
            r3_copy(l, k).wait_send()

    for copy in state_out:
        copy.wait()
    for l in range(layers):
        grad_out(l).wait()


def fast_body(ket_state, bra_state, gates, targets, swap_order):
    layers, gate_count, _, width, _ = gates.shape
    n_lo, n_hi = lax.axis_size("lo"), lax.axis_size("hi")
    amps = ket_state.shape[1]
    chunks = amps // (width * width)
    unit = width // n_lo
    half = gate_count // 2
    n_chip = n_lo // 2
    rows = width // n_hi
    piece = rows // n_chip
    scale = (amps * n_lo * n_hi // width) ** (-0.5)
    shape = (chunks, 2, n_lo, unit, 2 * width)
    flat = (2 * amps // width, width)

    def as_rows(v):
        return v.reshape(2, amps // width, width).transpose(1, 0, 2).reshape(-1, width)

    def from_rows(v):
        return v.reshape(amps // width, 2, width).transpose(1, 0, 2).reshape(2, amps)

    dma = pltpu.SemaphoreType.DMA
    ket_out, bra_out, grads = pl.pallas_call(
        functools.partial(kernel, n_hi, n_lo, layers, gate_count, chunks, width, scale),
        out_shape=(
            jax.ShapeDtypeStruct(flat, f32),
            jax.ShapeDtypeStruct(flat, f32),
            jax.ShapeDtypeStruct((layers, gate_count, 2, n_chip, piece, width), f32),
        ),
        in_specs=[
            pl.BlockSpec(memory_space=pltpu.SMEM),
            pl.BlockSpec(memory_space=pl.ANY),
            pl.BlockSpec(memory_space=pl.ANY),
            pl.BlockSpec(memory_space=pl.ANY),
            pl.BlockSpec(memory_space=pltpu.VMEM),
        ],
        out_specs=[pl.BlockSpec(memory_space=pl.ANY)] * 3,
        scratch_shapes=[
            pltpu.VMEM(flat, f32),
            pltpu.VMEM(flat, f32),
            pltpu.VMEM((layers + 1,) + shape, f32),
            pltpu.VMEM((layers, chunks, n_lo, 2, unit, 2 * width), f32),
            pltpu.VMEM(shape, f32),
            pltpu.VMEM((layers, gate_count, 2 * width, 6 * width), bf16),
            pltpu.VMEM((gate_count, 2, 2 * width, chunks * width), bf16),
            pltpu.VMEM((half, 2, chunks * width, 2 * width), bf16),
            pltpu.VMEM((half, 2, 2 * width, chunks * width), bf16),
            pltpu.VMEM((layers, gate_count, 2, width, width), f32),
            pltpu.VMEM((layers, half, 2, width, width), f32),
            pltpu.VMEM((layers, half, 2, n_hi, n_chip, piece, width), f32),
            pltpu.VMEM((layers, n_hi, half, 2, n_chip, piece, width), f32),
            pltpu.VMEM((layers, half, 2, n_chip, piece, width), f32),
            pltpu.VMEM((layers, n_chip, half, 2, piece, width), f32),
            pltpu.VMEM((layers, n_chip, half, 2, n_hi, piece, width), f32),
            pltpu.VMEM((layers, half, 2, n_hi, piece, width), f32),
            pltpu.VMEM((layers, n_hi, half, 2, piece, width), f32),
            pltpu.VMEM((layers, gate_count, 2, n_chip, piece, width), f32),
            pltpu.VMEM(gates.shape, f32),
            dma((4,)), dma((2 + layers,)),
            dma((2, n_lo)), dma((2, n_lo)),
            dma((layers, chunks)), dma((layers, chunks)),
            dma((chunks, n_lo)), dma((chunks, n_lo)),
            dma((layers,)), dma((layers,)),
            dma((layers, n_hi)), dma((layers, n_hi)),
            dma((layers, n_chip)), dma((layers, n_chip)),
            dma((layers, n_lo)), dma((layers, n_lo)),
        ],
        compiler_params=pltpu.CompilerParams(
            collective_id=0, has_side_effects=True, vmem_limit_bytes=56 * 1024 * 1024
        ),
    )(swap_order, as_rows(ket_state), as_rows(bra_state), gates, targets[:, :, None, :])
    return (
        from_rows(ket_out),
        from_rows(bra_out),
        grads.reshape(layers, gate_count, 2, rows, width),
    )


exact_mode = lax.Precision.HIGHEST


def relabel(gate_matrix, ordering):
    gate_width = gate_matrix.shape[-1]
    picker = (ordering[:, None] == jnp.arange(gate_width, dtype=jnp.int32)[None, :]).astype(
        jnp.float32
    )
    return jnp.einsum("ik,ckl,jl->cij", picker, gate_matrix, picker, precision=exact_mode)


def right_apply(amplitudes, gate_matrix):
    real_part = jnp.einsum(
        "...j,ij->...i", amplitudes[0], gate_matrix[0], precision=exact_mode
    ) - jnp.einsum("...j,ij->...i", amplitudes[1], gate_matrix[1], precision=exact_mode)
    imag_part = jnp.einsum(
        "...j,ij->...i", amplitudes[0], gate_matrix[1], precision=exact_mode
    ) + jnp.einsum("...j,ij->...i", amplitudes[1], gate_matrix[0], precision=exact_mode)
    return jnp.stack([real_part, imag_part])


def left_apply(amplitudes, gate_matrix):
    real_part = jnp.einsum(
        "ij,djr->dir", gate_matrix[0], amplitudes[0], precision=exact_mode
    ) - jnp.einsum("ij,djr->dir", gate_matrix[1], amplitudes[1], precision=exact_mode)
    imag_part = jnp.einsum(
        "ij,djr->dir", gate_matrix[1], amplitudes[0], precision=exact_mode
    ) + jnp.einsum("ij,djr->dir", gate_matrix[0], amplitudes[1], precision=exact_mode)
    return jnp.stack([real_part, imag_part])


def low_grad(bra_view, ket_view):
    real_part = jnp.einsum(
        "ri,rj->ij", bra_view[0], ket_view[0], precision=exact_mode
    ) + jnp.einsum("ri,rj->ij", bra_view[1], ket_view[1], precision=exact_mode)
    imag_part = jnp.einsum(
        "ri,rj->ij", bra_view[1], ket_view[0], precision=exact_mode
    ) - jnp.einsum("ri,rj->ij", bra_view[0], ket_view[1], precision=exact_mode)
    return jnp.stack([real_part, imag_part])


def high_grad(bra_view, ket_view):
    real_part = jnp.einsum(
        "dir,djr->ij", bra_view[0], ket_view[0], precision=exact_mode
    ) + jnp.einsum("dir,djr->ij", bra_view[1], ket_view[1], precision=exact_mode)
    imag_part = jnp.einsum(
        "dir,djr->ij", bra_view[1], ket_view[0], precision=exact_mode
    ) - jnp.einsum("dir,djr->ij", bra_view[0], ket_view[1], precision=exact_mode)
    return jnp.stack([real_part, imag_part])


def advance(ket_state, bra_state, gate_matrix, kind, devices):
    gate_width = gate_matrix.shape[-1]
    if kind == 0:
        ket_view = ket_state.reshape(2, -1, gate_width)
        bra_view = bra_state.reshape(2, -1, gate_width)
        ket_next = right_apply(ket_view, gate_matrix)
        gradient = low_grad(bra_view, ket_next)
        bra_next = right_apply(bra_view, gate_matrix)
    else:
        ket_view = ket_state.reshape(2, devices, gate_width, -1)
        bra_view = bra_state.reshape(2, devices, gate_width, -1)
        ket_next = left_apply(ket_view, gate_matrix)
        gradient = high_grad(bra_view, ket_next)
        bra_next = left_apply(bra_view, gate_matrix)
    return (ket_next.reshape(ket_state.shape), bra_next.reshape(bra_state.shape), gradient)


def swap_states(ket_state, bra_state, ordering, block_count):
    outgoing = (
        jnp.take(ket_state.reshape(2, block_count, -1), ordering, axis=1),
        jnp.take(bra_state.reshape(2, block_count, -1), ordering, axis=1),
    )
    ket_incoming, bra_incoming = (
        lax.all_to_all(outgoing[0], "lo", split_axis=1, concat_axis=1, tiled=True),
        lax.all_to_all(outgoing[1], "lo", split_axis=1, concat_axis=1, tiled=True),
    )
    return (ket_incoming.reshape(ket_state.shape), bra_incoming.reshape(bra_state.shape))


def swap_with_gate(ket_state, bra_state, ordering, gate_matrix, block_count):
    gate_width = gate_matrix.shape[-1]
    ket_outgoing = jnp.take(ket_state.reshape(2, block_count, -1), ordering, axis=1).reshape(
        2, block_count, -1, gate_width
    )
    bra_outgoing = jnp.take(bra_state.reshape(2, block_count, -1), ordering, axis=1).reshape(
        2, block_count, -1, gate_width
    )
    ket_piece = lax.all_to_all(ket_outgoing, "lo", split_axis=1, concat_axis=1, tiled=True)
    bra_piece = lax.all_to_all(bra_outgoing, "lo", split_axis=1, concat_axis=1, tiled=True)
    return (right_apply(ket_piece, gate_matrix), bra_piece, right_apply(bra_piece, gate_matrix))


def body(ket_state, bra_state, gates, targets, swap_order):
    gate_width = gates.shape[-1]
    layer_count = gates.shape[0]
    gate_count = gates.shape[1]
    block_count = lax.axis_size("lo")
    group_count = lax.axis_size("hi")
    amp_count = ket_state.shape[1]
    grad_scale = (amp_count * block_count * group_count // gate_width) ** (-0.5)
    row_count = gate_width // group_count
    collected = []
    carried = None
    for layer_index in range(layer_count):
        gradients = []
        for gate_index in range(gate_count):
            if carried is not None and gate_index == 0:
                ket_arrived, bra_before, bra_arrived = carried
                gradient = low_grad(
                    bra_before.reshape(2, -1, gate_width), ket_arrived.reshape(2, -1, gate_width)
                )
                ket_state = ket_arrived.reshape(2, amp_count)
                bra_state = bra_arrived.reshape(2, amp_count)
                carried = None
            else:
                gate_matrix = relabel(
                    gates[layer_index, gate_index], targets[layer_index, gate_index]
                )
                ket_state, bra_state, gradient = advance(
                    ket_state, bra_state, gate_matrix, gate_index % 2, 1
                )
            gradients.append(gradient * grad_scale)
        stacked = jnp.stack(gradients)
        summed = lax.psum(stacked, ("hi", "lo"))
        collected.append(
            lax.dynamic_slice_in_dim(summed, lax.axis_index("hi") * row_count, row_count, 2)
        )
        if layer_index + 1 < layer_count:
            next_gate = relabel(gates[layer_index + 1, 0], targets[layer_index + 1, 0])
            carried = swap_with_gate(
                ket_state, bra_state, swap_order[layer_index], next_gate, block_count
            )
        else:
            ket_state, bra_state = swap_states(
                ket_state, bra_state, swap_order[layer_index], block_count
            )
    all_grads = jnp.stack(collected)
    return (ket_state, bra_state, all_grads)


def solution(mesh):
    specs = dict(
        mesh=mesh,
        in_specs=(P(None, ("hi", "lo")), P(None, ("hi", "lo")), P(), P(), P()),
        out_specs=(P(None, ("hi", "lo")), P(None, ("hi", "lo")), P(None, None, None, "hi", None)),
        check_vma=False,
    )

    def run(ket_state, bra_state, gates, targets, swap_order):
        n_hi, n_lo = mesh.shape["hi"], mesh.shape["lo"]
        _, gate_count, _, width, _ = gates.shape
        chunks = ket_state.shape[1] // (n_hi * n_lo * width * width)
        fits = (
            width % (8 * n_lo) == 0
            and n_lo % 2 == 0
            and width % (4 * n_hi * n_lo) == 0
            and gate_count % 2 == 0
            and chunks == n_lo // 2
            and chunks in (4, 8, 16)
            and gates.shape[0] >= 4
        )
        chosen = fast_body if fits else body
        return jax.shard_map(chosen, **specs)(ket_state, bra_state, gates, targets, swap_order)

    return run
```

```python
import functools

import jax
import jax.numpy as jnp
from jax import lax
from jax.experimental import pallas as pl
from jax.experimental.pallas import tpu as pltpu
from jax.sharding import PartitionSpec as P

bf16 = jnp.bfloat16
f32 = jnp.float32


def split(x):
    high = x.astype(bf16)
    return high, (x - high.astype(f32)).astype(bf16)


def mm(a, b):
    return lax.dot_general(a, b, (((1,), (0,)), ((), ())), preferred_element_type=f32)


def mm_nt(a, b):
    return lax.dot_general(a, b, (((1,), (1,)), ((), ())), preferred_element_type=f32)


def block_swap(x):
    r, c = x.shape[0] // 2, x.shape[1] // 2
    return jnp.concatenate(
        [
            jnp.concatenate([x[:r, :c], x[r:, :c]], axis=1),
            jnp.concatenate([x[:r, c:], x[r:, c:]], axis=1),
        ],
        axis=0,
    )


def kernel(
    n_hi, n_lo, layers, gate_count, chunks, width, scale,
    sigma_ref, ket_hbm, bra_hbm, gates_hbm, targets_ref, ket_out, bra_out, grad_hbm,
    ket_ref, bra_ref, rbuf, sbuf, ybuf, vbuf, tape_b, tape_even, tape_odd,
    acc, r0buf, hsum, r1buf, p1, r2buf, x1buf, x2, x2buf, gout,
    gates_ref, in_sem, out_sem, gather_s, gather_r, trade_s, trade_r, home_s, home_r,
    s0, q0, s1, q1, s2, q2, s3, q3,
):
    h = lax.axis_index("hi")
    q = lax.axis_index("lo")
    core = lax.rem(q, 2)
    chip = q // 2
    n_chip = n_lo // 2
    half = gate_count // 2
    rows = width // n_hi
    piece = rows // n_chip
    w2 = 2 * width
    last = layers - 1

    def lo_peer(k):
        return lax.rem(q + k, n_lo)

    def hi_peer(k):
        return lax.rem(h + k, n_hi)

    def chip_peer(k):
        peer, bit = 0, 1
        while bit < n_chip:
            own = lax.rem(chip // bit, 2)
            peer = peer + bit * (1 - own if k & bit else own)
            bit *= 2
        return peer

    in_copies = [
        pltpu.make_async_copy(gates_hbm.at[0], gates_ref.at[0], in_sem.at[0]),
        pltpu.make_async_copy(ket_hbm, ket_ref, in_sem.at[1]),
        pltpu.make_async_copy(bra_hbm, bra_ref, in_sem.at[2]),
        pltpu.make_async_copy(
            gates_hbm.at[pl.ds(1, last)], gates_ref.at[pl.ds(1, last)], in_sem.at[3]
        ),
    ]
    for copy in in_copies:
        copy.start()

    barrier = pltpu.get_barrier_semaphore()
    for k in range(1, n_lo):
        pl.semaphore_signal(barrier, inc=1, device_id={"lo": lo_peer(k)})
    for k in range(1, n_hi):
        pl.semaphore_signal(barrier, inc=1, device_id={"hi": hi_peer(k)})

    def entering(m):
        parts = [
            jnp.concatenate(
                [v[pl.ds(2 * m + c, width, stride=2 * chunks), :] for v in (ket_ref, bra_ref)], axis=1
            )
            for c in range(2)
        ]
        return jnp.concatenate(parts, axis=0)

    def prepare(layer, gate):
        order = targets_ref[layer, gate]
        picks = (
            jnp.broadcast_to(order, (width, width))
            == lax.broadcasted_iota(jnp.int32, (width, width), 0)
        ).astype(f32)
        rows_pick = picks.T.astype(bf16)
        g = gates_ref[layer, gate]
        rh, rl = split(g[0])
        ih, il = split(g[1])
        t = mm(jnp.concatenate([rh, ih, rl, il], axis=0), picks.astype(bf16)).astype(bf16)
        w = mm(
            rows_pick,
            jnp.concatenate([t[i * width:(i + 1) * width] for i in range(4)], axis=1),
        ).astype(bf16)
        wrh, wih, wrl, wil = [w[:, i * width:(i + 1) * width] for i in range(4)]
        vbuf[layer, gate] = jnp.concatenate(
            [
                jnp.concatenate([wrh, -wih, wrh, -wih, wrl, -wil], axis=1),
                jnp.concatenate([wih, wrh, wih, wrh, wil, wrl], axis=1),
            ],
            axis=0,
        )

    chip_order = list(range(n_chip - 1, -1, -1))
    targets_order = [(kc, ke) for kc in chip_order for ke in (1, 0)]
    others = [pair for pair in targets_order if pair != (0, 0)]
    part = chunks // 2

    def gather_copy(kc, ke, p, incoming=False):
        m, e = chip_peer(kc), lax.rem(core + ke, 2)
        d = 2 * m + e
        return pltpu.make_async_remote_copy(
            src_ref=sbuf.at[0, m, pl.ds(chunks * e + part * p, part)],
            dst_ref=rbuf.at[1, pl.ds(part * p, part), :, d if incoming else q],
            send_sem=gather_s.at[p, d],
            recv_sem=gather_r.at[p, d if incoming else q],
            device_id={"lo": d},
        )

    def trade_copy(l, i, incoming=False):
        return pltpu.make_async_remote_copy(
            src_ref=sbuf.at[l, i, pl.ds(0, chunks)],
            dst_ref=rbuf.at[l + 1, :, :, 2 * i + (1 - core if incoming else core)],
            send_sem=trade_s.at[l, i],
            recv_sem=trade_r.at[l, i],
            device_id={"lo": q + 1 - 2 * core},
        )

    def home_copy(i, kc, ke, incoming=False):
        m, e = chip_peer(kc), lax.rem(core + ke, 2)
        d = 2 * m + e
        return pltpu.make_async_remote_copy(
            src_ref=sbuf.at[last, i, d],
            dst_ref=rbuf.at[layers, m if incoming else chip, :, 2 * i + (e if incoming else core)],
            send_sem=home_s.at[i, d],
            recv_sem=home_r.at[i, d if incoming else q],
            device_id={"lo": d},
        )

    def r0_copy(l):
        return pltpu.make_async_remote_copy(
            src_ref=acc.at[l, pl.ds(half * (1 - core), half)],
            dst_ref=r0buf.at[l],
            send_sem=s0.at[l],
            recv_sem=q0.at[l],
            device_id={"lo": q + 1 - 2 * core},
        )

    lo_first = (1,)

    def hi_copy(l, k, incoming=False):
        d = hi_peer(k)
        if l in lo_first:
            src, dst = x2.at[l, :, :, d], x2buf.at[l, d if incoming else h]
        else:
            src, dst = hsum.at[l, :, :, d], r1buf.at[l, d if incoming else h]
        return pltpu.make_async_remote_copy(
            src_ref=src,
            dst_ref=dst,
            send_sem=s1.at[l, d],
            recv_sem=q1.at[l, d if incoming else h],
            device_id={"hi": d},
        )

    def chip_copy(l, k, incoming=False):
        d = chip_peer(k)
        if l in lo_first:
            src, dst = hsum.at[l, :, :, :, d], x1buf.at[l, d if incoming else chip]
        else:
            src, dst = p1.at[l, :, :, d], r2buf.at[l, d if incoming else chip]
        return pltpu.make_async_remote_copy(
            src_ref=src,
            dst_ref=dst,
            send_sem=s2.at[l, d],
            recv_sem=q2.at[l, d if incoming else chip],
            device_id={"lo": 2 * d + core},
        )

    def r3_copy(l, k, incoming=False):
        d = lo_peer(k)
        owner = d if incoming else q
        place = gout.at[l, pl.ds(half * lax.rem(owner, 2), half), :, owner // 2]
        return pltpu.make_async_remote_copy(
            src_ref=place,
            dst_ref=place,
            send_sem=s3.at[l, d],
            recv_sem=q3.at[l, owner],
            device_id={"lo": d},
        )

    def hi_start(l):
        for k in range(n_hi - 1, 0, -1):
            hi_copy(l, k).start()

    def chip_start(l):
        for k in range(n_chip - 1, 0, -1):
            chip_copy(l, k).start()

    def stage0(l):
        r0_copy(l).wait_recv()
        total = acc[l, pl.ds(half * core, half)] + r0buf[l]
        hsum[l] = total.reshape(half, 2, n_hi, n_chip, piece, width)
        if l in lo_first:
            chip_start(l)
        else:
            hi_start(l)

    def stage1(l):
        if l in lo_first:
            total = hsum[l, :, :, :, chip]
            for k in range(1, n_chip):
                chip_copy(l, k, True).wait_recv()
                total = total + x1buf[l, chip_peer(k)]
            x2[l] = total
            hi_start(l)
        else:
            total = hsum[l, :, :, h]
            for k in range(1, n_hi):
                hi_copy(l, k, True).wait_recv()
                total = total + r1buf[l, hi_peer(k)]
            p1[l] = total
            chip_start(l)

    def stage2(l):
        if l in lo_first:
            total = x2[l, :, :, h]
            for k in range(1, n_hi):
                hi_copy(l, k, True).wait_recv()
                total = total + x2buf[l, hi_peer(k)]
        else:
            total = p1[l, :, :, chip]
            for k in range(1, n_chip):
                chip_copy(l, k, True).wait_recv()
                total = total + r2buf[l, chip_peer(k)]
        gout[l, pl.ds(half * core, half), :, chip] = total * scale
        for k in range(n_lo - 1, 0, -1):
            r3_copy(l, k).start()

    def grad_out(l):
        return pltpu.make_async_copy(gout.at[l], grad_hbm.at[l], out_sem.at[2 + l])

    def stage3(l):
        for k in range(1, n_lo):
            r3_copy(l, k, True).wait_recv()
        grad_out(l).start()

    def cat(v, axis):
        return jnp.concatenate(v, axis=axis) if len(v) > 1 else v[0]

    def apply_gates(ss, l, first):
        n = len(ss)
        hs, ls = zip(*[split(s) for s in ss])
        spans = [slice((first + i) * width, (first + i + 1) * width) for i in range(n)]
        for g in range(gate_count):
            v = vbuf[l, g]
            if g % 2 == 0:
                xh = cat([block_swap(t) for t in hs], 0)
                xl = cat([block_swap(t) for t in ls], 0)
                y = mm_nt(cat([xh, xl, xh], 1), v)
                ys = [y[i * w2:(i + 1) * w2] for i in range(n)]
                yhs, yls = zip(*[split(t) for t in ys])
                for s, yh, yl, span in zip(ss, yhs, yls, spans):
                    bh, bl = split(cat([s[:width, width:], s[width:, width:]], 1).T)
                    tape_b[g, 0, :, span] = bh
                    tape_b[g, 1, :, span] = bl
                    tape_even[g // 2, 0, span, :] = yh[:width]
                    tape_even[g // 2, 1, span, :] = yl[:width]
                ss = [block_swap(t) for t in ys]
                hs = [block_swap(t) for t in yhs]
                ls = [block_swap(t) for t in yls]
            else:
                sh, sl = cat(hs, 1), cat(ls, 1)
                y = mm(v, cat([sh, sl, sh], 0))
                ys = [y[:, i * w2:(i + 1) * w2] for i in range(n)]
                yhs, yls = zip(*[split(t) for t in ys])
                for sh, sl, yh, yl, span in zip(hs, ls, yhs, yls, spans):
                    tape_b[g, 0, :, span] = sh[:, width:]
                    tape_b[g, 1, :, span] = sl[:, width:]
                    tape_odd[g // 2, 0, :, span] = yh[:, :width]
                    tape_odd[g // 2, 1, :, span] = yl[:, :width]
                ss, hs, ls = ys, yhs, yls
        return ss

    def gradients(l):
        @pl.loop(0, half)
        def _(pair):
            for odd in range(2):
                g = 2 * pair + odd
                bh, bl = tape_b[g, 0], tape_b[g, 1]
                b = cat([bh, bh, bl], 1)
                if odd:
                    kh, kl = tape_odd[pair, 0], tape_odd[pair, 1]
                    grad = mm_nt(b, cat([kh, kl, kh], 1))
                else:
                    kh, kl = tape_even[pair, 0], tape_even[pair, 1]
                    grad = mm(b, cat([kh, kl, kh], 0))
                acc[l, g, 0] = grad[:width, :width] + grad[width:, width:]
                acc[l, g, 1] = grad[width:, :width] - grad[:width, width:]

        r0_copy(l).start()

    def load(l, i):
        return rbuf[l, i].reshape(w2, w2)

    in_copies[0].wait()
    for g in range(gate_count):
        prepare(0, g)
    in_copies[1].wait()
    in_copies[2].wait()
    done = 0
    for todo in (chip_order[:1], chip_order[1:]):
        states = apply_gates([entering(chip_peer(kc)) for kc in todo], 0, done)
        done += len(todo)
        for kc, state in zip(todo, states):
            ybuf[kc] = state.reshape(ybuf.shape[1:])
        if todo[0] == chip_order[0]:
            pl.semaphore_wait(barrier, n_lo - 1 + n_hi - 1)
        for p in range(2):
            for kc in todo:
                m = chip_peer(kc)
                for ke in (1, 0):
                    e = lax.rem(core + ke, 2)
                    for j in range(part * p, part * (p + 1)):
                        block = ybuf[kc, :, sigma_ref[0, 2 * j + e]]
                        if (kc, ke) == (0, 0):
                            rbuf[1, j, :, q] = block
                        else:
                            sbuf[0, m, chunks * e + j] = block
                    if (kc, ke) != (0, 0):
                        gather_copy(kc, ke, p).start()
    gradients(0)
    in_copies[3].wait()

    def prepare_layers(first, end):
        @pl.loop(first, end)
        def _(l):
            for g in range(gate_count):
                prepare(l, g)

    prepare_layers(1, 2)
    stage0(0)
    prepare_layers(2, layers)

    for l in range(1, last):
        for p in range(2):
            if l == 1:
                for kc, ke in others:
                    gather_copy(kc, ke, p, True).wait_recv()
            elif p == 0:
                for i in range(chunks):
                    trade_copy(l - 1, i, True).wait_recv()
            todo = range(part * p, part * (p + 1))
            states = apply_gates([load(l, i) for i in todo], l, part * p)
            for i, state in zip(todo, states):
                ybuf[i] = state.reshape(ybuf.shape[1:])
                for j in range(chunks):
                    sbuf[l, i, j] = ybuf[i, :, sigma_ref[l, 2 * j + 1 - core]]
                trade_copy(l, i).start()
                for j in range(chunks):
                    rbuf[l + 1, j, :, 2 * i + core] = ybuf[i, :, sigma_ref[l, 2 * j + core]]
            if l > 1 and p == 0:
                stage0(l - 1)
        if l == 1:
            stage1(0)
        else:
            stage2(l - 2)
            if l - 1 not in lo_first:
                stage1(l - 1)
        gradients(l)
        if l > 1 and l - 1 in lo_first and l + 1 < last:
            stage1(l - 1)

    for i in range(chunks):
        trade_copy(last - 1, i, True).wait_recv()
    for todo in ([0], range(1, chunks)):
        states = apply_gates([load(last, i) for i in todo], last, todo[0])
        for i, state in zip(todo, states):
            ybuf[i] = state.reshape(ybuf.shape[1:])
            for kc, ke in targets_order:
                d = 2 * chip_peer(kc) + lax.rem(core + ke, 2)
                block = ybuf[i, :, sigma_ref[last, d]]
                if (kc, ke) == (0, 0):
                    rbuf[layers, chip, :, 2 * i + core] = block
                else:
                    sbuf[last, i, d] = block
                    home_copy(i, kc, ke).start()
        if todo[0] == 0:
            stage0(last - 1)
    gradients(last)
    if last - 2 in lo_first:
        stage1(last - 2)
    stage0(last)
    stage2(last - 2)
    stage1(last - 1)
    for l in range(last - 2):
        stage3(l)

    for kc in [0] + [k for k in chip_order if k]:
        for ke in (1, 0):
            if (kc, ke) != (0, 0):
                for i in range(chunks):
                    home_copy(i, kc, ke, True).wait_recv()
        m = chip_peer(kc)
        state = load(layers, m)
        for c in range(2):
            for n, out in enumerate((ket_out, bra_out)):
                out[pl.ds(2 * m + c, width, stride=2 * chunks), :] = state[
                    c * width:(c + 1) * width, n * width:(n + 1) * width
                ]
    stage1(last)
    stage2(last - 1)
    stage2(last)
    for l in range(last - 2, layers):
        stage3(l)

    for kc, ke in others:
        for p in range(2):
            gather_copy(kc, ke, p).wait_send()

    @pl.loop(0, chunks)
    def _(i):
        for kc, ke in others:
            home_copy(i, kc, ke).wait_send()

        @pl.loop(1, last)
        def _(l):
            trade_copy(l, i).wait_send()

    for l in range(layers):
        r0_copy(l).wait_send()
        for k in range(1, n_hi):
            hi_copy(l, k).wait_send()
        for k in range(1, n_chip):
            chip_copy(l, k).wait_send()
        for k in range(1, n_lo):
            r3_copy(l, k).wait_send()

    for l in range(layers):
        grad_out(l).wait()


def hand_over(ket_in, bra_in, grad_in, ket_out, bra_out, grad_out, put):
    pairs = ((ket_in, ket_out), (bra_in, bra_out), (grad_in, grad_out))
    ways = [pltpu.make_async_copy(src, dst, put.at[n]) for n, (src, dst) in enumerate(pairs)]
    for way in ways:
        way.start()
    for way in ways:
        way.wait()


def fast_body(ket_state, bra_state, gates, targets, swap_order):
    layers, gate_count, _, width, _ = gates.shape
    n_lo, n_hi = lax.axis_size("lo"), lax.axis_size("hi")
    amps = ket_state.shape[1]
    chunks = amps // (width * width)
    unit = width // n_lo
    half = gate_count // 2
    n_chip = n_lo // 2
    rows = width // n_hi
    piece = rows // n_chip
    scale = (amps * n_lo * n_hi // width) ** (-0.5)
    shape = (chunks, 2, n_lo, unit, 2 * width)
    flat = (2 * amps // width, width)

    def as_rows(v):
        return v.reshape(2, amps // width, width).transpose(1, 0, 2).reshape(-1, width)

    def from_rows(v):
        return v.reshape(amps // width, 2, width).transpose(1, 0, 2).reshape(2, amps)

    dma = pltpu.SemaphoreType.DMA
    ket_out, bra_out, grads = pl.pallas_call(
        functools.partial(kernel, n_hi, n_lo, layers, gate_count, chunks, width, scale),
        out_shape=(
            pltpu.VMEM(flat, f32),
            pltpu.VMEM(flat, f32),
            pltpu.VMEM((layers, gate_count, 2, n_chip, piece, width), f32),
        ),
        in_specs=[
            pl.BlockSpec(memory_space=pltpu.SMEM),
            pl.BlockSpec(memory_space=pl.ANY),
            pl.BlockSpec(memory_space=pl.ANY),
            pl.BlockSpec(memory_space=pl.ANY),
            pl.BlockSpec(memory_space=pltpu.VMEM),
        ],
        out_specs=[pl.BlockSpec(memory_space=pltpu.VMEM)] * 3,
        scratch_shapes=[
            pltpu.VMEM(flat, f32),
            pltpu.VMEM(flat, f32),
            pltpu.VMEM((layers + 1,) + shape, f32),
            pltpu.VMEM((layers, chunks, n_lo, 2, unit, 2 * width), f32),
            pltpu.VMEM(shape, f32),
            pltpu.VMEM((layers, gate_count, 2 * width, 6 * width), bf16),
            pltpu.VMEM((gate_count, 2, 2 * width, chunks * width), bf16),
            pltpu.VMEM((half, 2, chunks * width, 2 * width), bf16),
            pltpu.VMEM((half, 2, 2 * width, chunks * width), bf16),
            pltpu.VMEM((layers, gate_count, 2, width, width), f32),
            pltpu.VMEM((layers, half, 2, width, width), f32),
            pltpu.VMEM((layers, half, 2, n_hi, n_chip, piece, width), f32),
            pltpu.VMEM((layers, n_hi, half, 2, n_chip, piece, width), f32),
            pltpu.VMEM((layers, half, 2, n_chip, piece, width), f32),
            pltpu.VMEM((layers, n_chip, half, 2, piece, width), f32),
            pltpu.VMEM((layers, n_chip, half, 2, n_hi, piece, width), f32),
            pltpu.VMEM((layers, half, 2, n_hi, piece, width), f32),
            pltpu.VMEM((layers, n_hi, half, 2, piece, width), f32),
            pltpu.VMEM((layers, gate_count, 2, n_chip, piece, width), f32),
            pltpu.VMEM(gates.shape, f32),
            dma((4,)), dma((2 + layers,)),
            dma((2, n_lo)), dma((2, n_lo)),
            dma((layers, chunks)), dma((layers, chunks)),
            dma((chunks, n_lo)), dma((chunks, n_lo)),
            dma((layers,)), dma((layers,)),
            dma((layers, n_hi)), dma((layers, n_hi)),
            dma((layers, n_chip)), dma((layers, n_chip)),
            dma((layers, n_lo)), dma((layers, n_lo)),
        ],
        compiler_params=pltpu.CompilerParams(
            collective_id=0, has_side_effects=True, vmem_limit_bytes=56 * 1024 * 1024
        ),
    )(swap_order, as_rows(ket_state), as_rows(bra_state), gates, targets[:, :, None, :])
    ket_out, bra_out, grads = pl.pallas_call(
        hand_over,
        out_shape=tuple(jax.ShapeDtypeStruct(v.shape, f32) for v in (ket_out, bra_out, grads)),
        in_specs=[pl.BlockSpec(memory_space=pltpu.VMEM)] * 3,
        out_specs=[pl.BlockSpec(memory_space=pl.ANY)] * 3,
        scratch_shapes=[dma((3,))],
        compiler_params=pltpu.CompilerParams(vmem_limit_bytes=4 * 1024 * 1024),
    )(ket_out, bra_out, grads)
    return (
        from_rows(ket_out),
        from_rows(bra_out),
        grads.reshape(layers, gate_count, 2, rows, width),
    )


exact_mode = lax.Precision.HIGHEST


def relabel(gate_matrix, ordering):
    gate_width = gate_matrix.shape[-1]
    picker = (ordering[:, None] == jnp.arange(gate_width, dtype=jnp.int32)[None, :]).astype(
        jnp.float32
    )
    return jnp.einsum("ik,ckl,jl->cij", picker, gate_matrix, picker, precision=exact_mode)


def right_apply(amplitudes, gate_matrix):
    real_part = jnp.einsum(
        "...j,ij->...i", amplitudes[0], gate_matrix[0], precision=exact_mode
    ) - jnp.einsum("...j,ij->...i", amplitudes[1], gate_matrix[1], precision=exact_mode)
    imag_part = jnp.einsum(
        "...j,ij->...i", amplitudes[0], gate_matrix[1], precision=exact_mode
    ) + jnp.einsum("...j,ij->...i", amplitudes[1], gate_matrix[0], precision=exact_mode)
    return jnp.stack([real_part, imag_part])


def left_apply(amplitudes, gate_matrix):
    real_part = jnp.einsum(
        "ij,djr->dir", gate_matrix[0], amplitudes[0], precision=exact_mode
    ) - jnp.einsum("ij,djr->dir", gate_matrix[1], amplitudes[1], precision=exact_mode)
    imag_part = jnp.einsum(
        "ij,djr->dir", gate_matrix[1], amplitudes[0], precision=exact_mode
    ) + jnp.einsum("ij,djr->dir", gate_matrix[0], amplitudes[1], precision=exact_mode)
    return jnp.stack([real_part, imag_part])


def low_grad(bra_view, ket_view):
    real_part = jnp.einsum(
        "ri,rj->ij", bra_view[0], ket_view[0], precision=exact_mode
    ) + jnp.einsum("ri,rj->ij", bra_view[1], ket_view[1], precision=exact_mode)
    imag_part = jnp.einsum(
        "ri,rj->ij", bra_view[1], ket_view[0], precision=exact_mode
    ) - jnp.einsum("ri,rj->ij", bra_view[0], ket_view[1], precision=exact_mode)
    return jnp.stack([real_part, imag_part])


def high_grad(bra_view, ket_view):
    real_part = jnp.einsum(
        "dir,djr->ij", bra_view[0], ket_view[0], precision=exact_mode
    ) + jnp.einsum("dir,djr->ij", bra_view[1], ket_view[1], precision=exact_mode)
    imag_part = jnp.einsum(
        "dir,djr->ij", bra_view[1], ket_view[0], precision=exact_mode
    ) - jnp.einsum("dir,djr->ij", bra_view[0], ket_view[1], precision=exact_mode)
    return jnp.stack([real_part, imag_part])


def advance(ket_state, bra_state, gate_matrix, kind, devices):
    gate_width = gate_matrix.shape[-1]
    if kind == 0:
        ket_view = ket_state.reshape(2, -1, gate_width)
        bra_view = bra_state.reshape(2, -1, gate_width)
        ket_next = right_apply(ket_view, gate_matrix)
        gradient = low_grad(bra_view, ket_next)
        bra_next = right_apply(bra_view, gate_matrix)
    else:
        ket_view = ket_state.reshape(2, devices, gate_width, -1)
        bra_view = bra_state.reshape(2, devices, gate_width, -1)
        ket_next = left_apply(ket_view, gate_matrix)
        gradient = high_grad(bra_view, ket_next)
        bra_next = left_apply(bra_view, gate_matrix)
    return (ket_next.reshape(ket_state.shape), bra_next.reshape(bra_state.shape), gradient)


def swap_states(ket_state, bra_state, ordering, block_count):
    outgoing = (
        jnp.take(ket_state.reshape(2, block_count, -1), ordering, axis=1),
        jnp.take(bra_state.reshape(2, block_count, -1), ordering, axis=1),
    )
    ket_incoming, bra_incoming = (
        lax.all_to_all(outgoing[0], "lo", split_axis=1, concat_axis=1, tiled=True),
        lax.all_to_all(outgoing[1], "lo", split_axis=1, concat_axis=1, tiled=True),
    )
    return (ket_incoming.reshape(ket_state.shape), bra_incoming.reshape(bra_state.shape))


def swap_with_gate(ket_state, bra_state, ordering, gate_matrix, block_count):
    gate_width = gate_matrix.shape[-1]
    ket_outgoing = jnp.take(ket_state.reshape(2, block_count, -1), ordering, axis=1).reshape(
        2, block_count, -1, gate_width
    )
    bra_outgoing = jnp.take(bra_state.reshape(2, block_count, -1), ordering, axis=1).reshape(
        2, block_count, -1, gate_width
    )
    ket_piece = lax.all_to_all(ket_outgoing, "lo", split_axis=1, concat_axis=1, tiled=True)
    bra_piece = lax.all_to_all(bra_outgoing, "lo", split_axis=1, concat_axis=1, tiled=True)
    return (right_apply(ket_piece, gate_matrix), bra_piece, right_apply(bra_piece, gate_matrix))


def body(ket_state, bra_state, gates, targets, swap_order):
    gate_width = gates.shape[-1]
    layer_count = gates.shape[0]
    gate_count = gates.shape[1]
    block_count = lax.axis_size("lo")
    group_count = lax.axis_size("hi")
    amp_count = ket_state.shape[1]
    grad_scale = (amp_count * block_count * group_count // gate_width) ** (-0.5)
    row_count = gate_width // group_count
    collected = []
    carried = None
    for layer_index in range(layer_count):
        gradients = []
        for gate_index in range(gate_count):
            if carried is not None and gate_index == 0:
                ket_arrived, bra_before, bra_arrived = carried
                gradient = low_grad(
                    bra_before.reshape(2, -1, gate_width), ket_arrived.reshape(2, -1, gate_width)
                )
                ket_state = ket_arrived.reshape(2, amp_count)
                bra_state = bra_arrived.reshape(2, amp_count)
                carried = None
            else:
                gate_matrix = relabel(
                    gates[layer_index, gate_index], targets[layer_index, gate_index]
                )
                ket_state, bra_state, gradient = advance(
                    ket_state, bra_state, gate_matrix, gate_index % 2, 1
                )
            gradients.append(gradient * grad_scale)
        stacked = jnp.stack(gradients)
        summed = lax.psum(stacked, ("hi", "lo"))
        collected.append(
            lax.dynamic_slice_in_dim(summed, lax.axis_index("hi") * row_count, row_count, 2)
        )
        if layer_index + 1 < layer_count:
            next_gate = relabel(gates[layer_index + 1, 0], targets[layer_index + 1, 0])
            carried = swap_with_gate(
                ket_state, bra_state, swap_order[layer_index], next_gate, block_count
            )
        else:
            ket_state, bra_state = swap_states(
                ket_state, bra_state, swap_order[layer_index], block_count
            )
    all_grads = jnp.stack(collected)
    return (ket_state, bra_state, all_grads)


def solution(mesh):
    specs = dict(
        mesh=mesh,
        in_specs=(P(None, ("hi", "lo")), P(None, ("hi", "lo")), P(), P(), P()),
        out_specs=(P(None, ("hi", "lo")), P(None, ("hi", "lo")), P(None, None, None, "hi", None)),
        check_vma=False,
    )

    def run(ket_state, bra_state, gates, targets, swap_order):
        n_hi, n_lo = mesh.shape["hi"], mesh.shape["lo"]
        _, gate_count, _, width, _ = gates.shape
        chunks = ket_state.shape[1] // (n_hi * n_lo * width * width)
        fits = (
            width % (8 * n_lo) == 0
            and n_lo % 2 == 0
            and width % (4 * n_hi * n_lo) == 0
            and gate_count % 2 == 0
            and chunks == n_lo // 2
            and chunks in (4, 8, 16)
            and gates.shape[0] >= 4
        )
        chosen = fast_body if fits else body
        return jax.shard_map(chosen, **specs)(ket_state, bra_state, gates, targets, swap_order)

    return run
```
